32 devices in a mesh: group: 2 (over x), reader: 16 (over z, y, core).
Axes of the slice: x: 2, y: 2, z: 4, core: 2. Of those that a mesh axis runs over, the one named last changes fastest.
Arguments:
- answer_lengths: int32 [64], P('group'), parts along dimension 0, may hold values from 1 to 256, 4096 in all
- mixer_input: bfloat16 [8192, 4096], P(('group', 'reader')), parts along dimension 0, may hold values from -6 to 6
- gate_input: bfloat16 [8192, 4096], P(('group', 'reader')), parts along dimension 0, may hold values from -6 to 6
- state_write: bfloat16 [8192, 512], P(('group', 'reader')), parts along dimension 0, may hold values from -6 to 6
- state_read: bfloat16 [8192, 512], P(('group', 'reader')), parts along dimension 0, may hold values from -0.5 to 0.5
- step_raw: float32 [8192, 64], P(('group', 'reader')), parts along dimension 0, may hold values from -4 to 50
- decay_rate: float32 [64], replicated, may hold values from 0.006 to 0.15
- skip_gain: float32 [64], replicated, may hold values from 0.5 to 2
- norm_gain: float32 [4096], replicated, may hold values from 0.1 to 1.9
- prompt_state: float32 [8192, 128], P(('group', 'reader')), parts along dimension 0, may hold values from -24 to 24
- queries: bfloat16 [8192, 2048], P(('group', 'reader')), parts along dimension 0, may hold values from -160 to 160
- answer_keys: bfloat16 [8192, 512], P(('group', 'reader')), parts along dimension 0, may hold values from -6 to 6
- answer_values: bfloat16 [8192, 512], P(('group', 'reader')), parts along dimension 0, may hold values from -48 to 48
- prompt_keys: bfloat16 [256, 512], P(('group', 'reader')), parts along dimension 0, may hold values from -4 to 4
- prompt_values: bfloat16 [256, 512], P(('group', 'reader')), parts along dimension 0, may hold values from -48 to 48
Outputs:
- mixer_out: bfloat16 [8192, 4096], P(('group', 'reader')), parts along dimension 0
- attention_out: bfloat16 [8192, 2048], P(('group', 'reader')), parts along dimension 0
The draws below stay inside these ranges and needn't reach their ends.
There are 2 independent parts, one for each index of `group`. The reference program is written for one: setup_inputs(seed, part) draws one part's arguments, and reference() takes and returns one part's arrays. A program takes and returns all parts, laid end to end along the dimension named above; an argument that names none is the same for every part. Nothing has to cross between parts.
Inputs may be any that keep to these rules, and one draw needn't show every extreme that they name: `answer_lengths`: the answers fill the 4096 tokens in order, back to back; the longest has exactly 256 tokens.
All inputs are finite; a program needn't handle non-finite values.
Results may differ from the reference program's by a relative error of at most 0.0047.
Values may be sent and summed in bfloat16 or wider, within the bound.
A program may use at most 128 MiB of HBM per device.

```python
import math
import jax
import jax.numpy as jnp
import numpy as np
from jax import lax

H = 64
P_SIZE = 64
N = 128
G = 4
QH = 16
KVH = 4
HD = 128
SPAN = 64
TOK_DEV = 256
PACKED_TOKENS = 4096
PROMPT = 128
ANSWERS = 32


def draw_step_raw(key, part):
    root_random_key, spike_random_key, level_random_key = jax.random.split(jax.random.fold_in(key, 1), 3)
    root_value_entry = jnp.clip(-1.2 + 0.5 * jax.random.normal(root_random_key, (PACKED_TOKENS, H), jnp.float32), -3.5, 0.5)
    spike_mask_rows = jax.random.bernoulli(spike_random_key, 1.0 / 256.0, (PACKED_TOKENS, 1))
    spike_level_value = jax.random.uniform(level_random_key, (PACKED_TOKENS, 1), jnp.float32, 30.0, 50.0)
    return jnp.where(spike_mask_rows, spike_level_value, root_value_entry).astype(jnp.float32)


def draw_decay_rate(key, part):
    spread_key = jax.random.fold_in(jax.random.fold_in(key, 2), 0)
    fraction = jax.random.uniform(spread_key, (H,), jnp.float32)
    return jnp.exp(math.log(0.006) + fraction * math.log(0.15 / 0.006)).astype(jnp.float32)


def prompt_table(key):
    return jnp.clip(jax.random.normal(jax.random.fold_in(key, 3), (PROMPT, KVH, HD), jnp.float32), -4.0, 4.0)


def draw_prompt_keys(key, part):
    key_table = prompt_table(key)
    return key_table.reshape(PROMPT, KVH * HD).astype(jnp.bfloat16)


def draw_queries(key, part):
    query_table = jnp.clip(jax.random.normal(jax.random.fold_in(key, 5), (PACKED_TOKENS, QH, HD), jnp.float32), -4.0, 4.0)
    return query_table.reshape(PACKED_TOKENS, QH * HD).astype(jnp.bfloat16)


def steps_of(rng, shape, cuts, least, high):
    def one(axis_at, parts):
        draws = jax.random.uniform(jax.random.fold_in(jax.random.fold_in(rng, 6), axis_at), (parts,), jnp.float32, least / len(cuts), high / len(cuts))
        return jnp.repeat(jnp.exp(draws), shape[axis_at] // parts).reshape((-1,) + (1,) * (len(shape) - axis_at - 1))

    level = one(*cuts[0])
    for cut in cuts[1:]:
        level = level * one(*cut)
    return level


def split_up(amount, total, limit, lean):
    loads = [(1 << 20) // math.isqrt(standing ** lean) + 1 for standing in range(2, amount + 1)]
    surplus, given = total - limit - (amount - 1), [1] * (amount - 1)
    while surplus > 0:
        movable = [i for i in range(amount - 1) if given[i] < limit]
        pool, left = sum([loads[i] for i in movable]), surplus
        for i in movable:
            extra = min(limit - given[i], max(1, left * loads[i] // pool), surplus)
            given[i] = given[i] + extra
            surplus = surplus - extra
    return np.array([limit] + given)


def ragged(rng, amount, total, most, lean):
    if amount == 2:
        one = jax.random.randint(rng, (), max(1, total - most), min(most, total - 1) + 1)
        return jnp.stack([one, total - one])
    sizes = jnp.asarray(split_up(amount, total, most, lean), jnp.int32)
    pairs = (amount - 1) // 2
    source_of, sink = sizes[1:1 + 2 * pairs:2], sizes[2:2 + 2 * pairs:2]
    slack = jnp.minimum(source_of - 1, most - sink)
    moved = jax.random.randint(jax.random.fold_in(rng, 1), (pairs,), 0, 1 << 20) % (slack + 1)
    sizes = sizes.at[1:1 + 2 * pairs:2].set(source_of - moved).at[2:2 + 2 * pairs:2].set(sink + moved)
    return sizes[jax.random.permutation(jax.random.fold_in(rng, 2), amount)]


def centred(stream_key, dims, scale, bound, shards=(), held_as=jnp.bfloat16):
    array = scale * jax.random.normal(stream_key, dims, jnp.float32)
    if shards:
        array = array * steps_of(stream_key, dims, shards, -0.22, 0.18)
    return jnp.clip(array, -bound, bound).astype(held_as)


def setup_inputs(seed: int = 0, part: int = 0) -> dict:
    streams_of = jax.random.split(jax.random.key(seed), 16)
    own_keys = jax.random.split(jax.random.fold_in(streams_of[15], part), 16)
    answer_lengths = ragged(own_keys[0], ANSWERS, PACKED_TOKENS, TOK_DEV, 1).astype(jnp.int32)
    mixer_input = centred(own_keys[1], (PACKED_TOKENS, H * P_SIZE), 1.0, 6.0, ((0, 16),))
    gate_input = centred(own_keys[2], (PACKED_TOKENS, H * P_SIZE), 1.0, 6.0, ((0, 16),))
    state_write = centred(own_keys[3], (PACKED_TOKENS, G * N), 1.0, 6.0, ((0, 16),))
    state_read = centred(own_keys[4], (PACKED_TOKENS, G * N), N ** -0.5, 0.5, ((0, 16),))
    step_raw = draw_step_raw(jax.random.fold_in(jax.random.fold_in(streams_of[15], part), 71), part)
    decay_rate = draw_decay_rate(jax.random.fold_in(streams_of[15], 71), part)
    skip_gain = jnp.clip(jax.random.uniform(streams_of[7], (H,), jnp.float32, 0.5, 2.0), 0.5, 2.0)
    norm_gain = jnp.clip(1.0 + 0.18 * jax.random.normal(streams_of[8], (H * P_SIZE,), jnp.float32), 0.1, 1.9)
    prompt_state = centred(own_keys[9], (H * P_SIZE, N), 4.0, 24.0, ((0, 16),), jnp.float32)
    queries = draw_queries(jax.random.fold_in(jax.random.fold_in(streams_of[15], part), 71), part)
    answer_keys = centred(own_keys[11], (PACKED_TOKENS, KVH * HD), 1.0, 6.0, ((0, 16),))
    answer_values = centred(own_keys[12], (PACKED_TOKENS, KVH * HD), 8.0, 48.0, ((0, 16),))
    prompt_keys = draw_prompt_keys(jax.random.fold_in(jax.random.fold_in(streams_of[15], part), 71), part)
    prompt_values = centred(own_keys[14], (PROMPT, KVH * HD), 8.0, 48.0, ((0, 16),))
    return {"answer_lengths": answer_lengths, "mixer_input": mixer_input, "gate_input": gate_input, "state_write": state_write, "state_read": state_read, "step_raw": step_raw, "decay_rate": decay_rate, "skip_gain": skip_gain, "norm_gain": norm_gain, "prompt_state": prompt_state, "queries": queries, "answer_keys": answer_keys, "answer_values": answer_values, "prompt_keys": prompt_keys, "prompt_values": prompt_values}


def segments_at(answer_lengths, places):
    answer_ends = jnp.cumsum(answer_lengths).astype(jnp.int32)
    answer_starts = (answer_ends - answer_lengths).astype(jnp.int32)
    segment = lax.optimization_barrier(jnp.sum((answer_ends[None, :] <= places[:, None]).astype(jnp.int32), axis=1)).astype(jnp.int32)
    numbers = jnp.arange(answer_lengths.shape[0], dtype=jnp.int32)
    start_of = lax.optimization_barrier(jnp.sum(jnp.where(segment[:, None] == numbers[None, :], answer_starts[None, :], 0), axis=1)).astype(jnp.int32)
    return (segment, (start_of == places).astype(jnp.int32))

def span_local(inputs_block, write_block, read_block, raw_block, segment, opening, decay_rate):
    length, groups, per_group, channels = inputs_block.shape
    step_size = jax.nn.softplus(raw_block)
    falling = -decay_rate[None, :] * step_size
    running = jnp.cumsum(falling, axis=0)
    before = running - falling
    places = jnp.arange(length, dtype=jnp.int32)
    same_answer = segment[:, None] == segment[None, :]
    leading = jnp.concatenate([jnp.ones((1,), dtype=bool), segment[1:] != segment[:-1]])
    entry_level = lax.optimization_barrier(jnp.sum(jnp.where((same_answer & leading[None, :])[:, :, None], before[None, :, :], 0.0), axis=1))
    decay_in = jnp.exp(running - entry_level)
    carried = same_answer[:, 0] & (opening[0] == 0)
    causal = same_answer & (places[None, :] <= places[:, None])
    spread = jnp.where(causal[:, :, None], running[:, None, :] - running[None, :, :], -jnp.inf)
    intersection = jnp.einsum('tgn,sgn->tsg', read_block.astype(jnp.float32), write_block.astype(jnp.float32))
    mixing = intersection[:, :, :, None] * jnp.exp(spread).reshape(length, length, groups, per_group) * step_size.reshape(1, length, groups, per_group)
    mixing = lax.optimization_barrier(mixing.astype(jnp.bfloat16)).astype(jnp.float32)
    inner_part = jnp.einsum('tsgk,sgkp->tgkp', mixing, inputs_block.astype(jnp.float32))
    closing = same_answer[length - 1].astype(jnp.float32)
    weight = jnp.exp(running[length - 1][None, :] - running) * step_size * closing[:, None]
    weighted = (inputs_block.astype(jnp.float32) * weight.reshape(length, groups, per_group, 1)).astype(jnp.bfloat16)
    weighted = lax.optimization_barrier(weighted).astype(jnp.float32)
    gathered_state = jnp.einsum('sgkp,sgn->gkpn', weighted, write_block.astype(jnp.float32))
    decay_end = jnp.exp(running[length - 1] - entry_level[length - 1]).reshape(groups, per_group)
    return (inner_part, decay_in, carried, gathered_state, decay_end, carried[length - 1])

def gated_norm(mixed_value, gate_input, norm_gain, groups):
    token_rows = mixed_value.shape[0]
    gated = mixed_value * jax.nn.silu(gate_input.astype(jnp.float32))
    grouped = gated.reshape(token_rows, groups, -1)
    mean_square = lax.optimization_barrier(jnp.mean(grouped * grouped, axis=2, keepdims=True))
    return (grouped * lax.rsqrt(mean_square + 1e-05)).reshape(token_rows, -1) * norm_gain[None, :]

def reference(answer_lengths, mixer_input, gate_input, state_write, state_read, step_raw, decay_rate, skip_gain, norm_gain, prompt_state, queries, answer_keys, answer_values, prompt_keys, prompt_values):
    per_group = H // G
    block_count = PACKED_TOKENS // SPAN
    places = jnp.arange(PACKED_TOKENS, dtype=jnp.int32)
    segment, opening = segments_at(answer_lengths, places)
    seed_state = prompt_state.reshape(G, per_group, P_SIZE, N)
    pieces = (mixer_input.reshape(block_count, SPAN, G, per_group, P_SIZE), state_write.reshape(block_count, SPAN, G, N), state_read.reshape(block_count, SPAN, G, N), step_raw.reshape(block_count, SPAN, H), segment.reshape(block_count, SPAN), opening.reshape(block_count, SPAN))

    def advance(carry_state, piece):
        inputs_block, write_block, read_block, raw_block, segment_block, opening_block = piece
        inner_part, decay_in, carried, gathered_state, decay_end, carried_last = span_local(inputs_block, write_block, read_block, raw_block, segment_block, opening_block, decay_rate)
        read_wide = read_block.astype(jnp.float32)
        from_prompt = jnp.einsum('tgn,gkpn->tgkp', read_wide, seed_state, precision=lax.Precision.HIGHEST)
        from_state = jnp.einsum('tgn,gkpn->tgkp', read_wide, carry_state, precision=lax.Precision.HIGHEST)
        inflow = jnp.where(carried[:, None, None, None], from_state, from_prompt) * decay_in.reshape(SPAN, G, per_group, 1)
        output = inner_part + inflow + skip_gain.reshape(1, G, per_group, 1) * inputs_block.astype(jnp.float32)
        entering = jnp.where(carried_last, carry_state, seed_state)
        return (decay_end[:, :, None, None] * entering + gathered_state, output)
    initial = jnp.zeros((G, per_group, P_SIZE, N), jnp.float32)
    final_state, outputs = lax.scan(advance, initial, pieces)
    mixer_out = gated_norm(outputs.reshape(PACKED_TOKENS, H * P_SIZE), gate_input, norm_gain, G).astype(jnp.bfloat16)
    group_size = QH // KVH
    score_scale = 1.0 / math.sqrt(HD)
    width = 512 + TOK_DEV
    cache_keys = prompt_keys.reshape(PROMPT, KVH, HD).astype(jnp.float32)
    cache_values = prompt_values.reshape(PROMPT, KVH, HD).astype(jnp.float32)

    def attend(block_index):
        row_start = (block_index * 512).astype(jnp.int32)
        key_start = jnp.maximum(row_start - TOK_DEV, 0).astype(jnp.int32)
        query_part = lax.dynamic_slice_in_dim(queries, row_start, 512, 0).reshape(512, KVH, group_size, HD).astype(jnp.float32)
        near_keys = lax.dynamic_slice_in_dim(answer_keys, key_start, width, 0).reshape(width, KVH, HD).astype(jnp.float32)
        near_values = lax.dynamic_slice_in_dim(answer_values, key_start, width, 0).reshape(width, KVH, HD).astype(jnp.float32)
        query_places = row_start + jnp.arange(512, dtype=jnp.int32)
        key_places = key_start + jnp.arange(width, dtype=jnp.int32)
        query_segment = lax.dynamic_slice_in_dim(segment, row_start, 512, 0)
        key_segment = lax.dynamic_slice_in_dim(segment, key_start, width, 0)
        allowed = (query_segment[:, None] == key_segment[None, :]) & (key_places[None, :] <= query_places[:, None])
        cache_scores = jnp.einsum('tkqd,skd->tkqs', query_part, cache_keys) * score_scale
        near_scores = jnp.einsum('tkqd,skd->tkqs', query_part, near_keys) * score_scale
        near_scores = jnp.where(allowed[:, None, None, :], near_scores, -jnp.inf)
        row_top = jnp.maximum(lax.optimization_barrier(jnp.max(cache_scores, axis=3)), lax.optimization_barrier(jnp.max(near_scores, axis=3)))
        cache_weights = jnp.exp(cache_scores - row_top[:, :, :, None])
        near_weights = jnp.exp(near_scores - row_top[:, :, :, None])
        weight_total = lax.optimization_barrier(jnp.sum(cache_weights, axis=3)) + lax.optimization_barrier(jnp.sum(near_weights, axis=3))
        cache_rounded = lax.optimization_barrier(cache_weights.astype(jnp.bfloat16)).astype(jnp.float32)
        near_rounded = lax.optimization_barrier(near_weights.astype(jnp.bfloat16)).astype(jnp.float32)
        summed = jnp.einsum('tkqs,skd->tkqd', cache_rounded, cache_values) + jnp.einsum('tkqs,skd->tkqd', near_rounded, near_values)
        return (summed / weight_total[:, :, :, None]).astype(jnp.bfloat16).reshape(512, QH * HD)
    attention_out = lax.map(attend, jnp.arange(PACKED_TOKENS // 512, dtype=jnp.int32)).reshape(PACKED_TOKENS, QH * HD)
    return (mixer_out, attention_out)
```

```python
import functools
import math

import jax
import jax.numpy as jnp
from jax import lax
from jax.experimental import pallas as pl
from jax.experimental.pallas import tpu as pltpu
from jax.sharding import PartitionSpec as P

HD = 128
F32 = jnp.float32
BF16 = jnp.bfloat16
MESH = pl.DeviceIdType.MESH
VMEM_LIMIT = 60 * 1024 * 1024


def iota(shape, axis):
    return lax.broadcasted_iota(jnp.int32, shape, axis)


def nt(a, b):
    return lax.dot_general(a, b, (((1,), (1,)), ((), ())), preferred_element_type=F32)


def starts_of_column(lengths_row, first, rows):
    n = lengths_row.shape[1]
    wide = jnp.broadcast_to(lengths_row.astype(F32), (8, n)).astype(BF16)
    ahead = (iota((n, n), 0) < iota((n, n), 1)).astype(F32).astype(BF16)
    starts = jnp.dot(wide, ahead, preferred_element_type=F32)[0:1, :]
    place = (iota((rows, n), 0) + first).astype(F32)
    return jnp.max(jnp.where(starts <= place, starts, -1.0), axis=1, keepdims=True)


def starts_of_row(lengths_row, first, columns):
    n = lengths_row.shape[1]
    wide = jnp.broadcast_to(lengths_row.astype(F32), (8, n)).astype(BF16)
    ahead = (iota((n, n), 1) < iota((n, n), 0)).astype(F32).astype(BF16)
    starts = nt(ahead, wide)[:, 0:1]
    place = (iota((n, columns), 1) + first).astype(F32)
    return jnp.max(jnp.where(starts <= place, starts, -1.0), axis=0, keepdims=True)


def column_of(value, index):
    lanes = iota(value.shape, 1)
    return jnp.sum(jnp.where(lanes == index, value, 0.0), axis=1, keepdims=True)


def pair_of(value, index, low):
    return jnp.where(low, column_of(value, index), column_of(value, index + 1))


def mix_kernel(
    readers, bits, groups,
    lengths, x, write, read, raw, rate, skip, prompt, pkeys, pvalues, keys, values,
    y_out, seed_out, pk_out, pv_out, d_prompt, d_state, prior_k, prior_v, prior_state,
    seed_buf, kv_buf, state_buf, tail_buf, tail_in, lo, lo_t, weight, write_t, inner,
    send, recv,
):
    rows = x.shape[0]
    heads = raw.shape[1]
    per_group = heads // groups
    size = write.shape[1] // groups
    pairs = x.shape[1] // 128
    pairs_per_group = pairs // groups
    me = lax.axis_index("reader")
    after = lax.rem(me + 1, readers)
    ahead = lax.rem(me + readers - 1, readers)
    partners = []
    slot = 0
    for step in range(bits):
        unit = 1 << (bits - 1 - step)
        bit = lax.rem(me // unit, 2)
        partners.append(me + unit * (1 - 2 * bit))
        slot = slot + bit * (1 << step)
    barrier = pltpu.get_barrier_semaphore()
    for other in partners + [after, ahead]:
        pl.semaphore_signal(barrier, inc=1, device_id={"reader": other}, device_id_type=MESH)
    seed_buf[slot] = prompt[...].astype(BF16)
    few = pkeys.shape[0]
    kv_buf[slot] = jnp.concatenate([pkeys[...], pvalues[...]], axis=0)
    pl.semaphore_wait(barrier, bits + 2)

    def remote(source, target, index, other):
        return pltpu.make_async_remote_copy(
            src_ref=source, dst_ref=target, send_sem=send.at[index], recv_sem=recv.at[index],
            device_id={"reader": other}, device_id_type=MESH,
        )

    def gather(step):
        count = 1 << step
        base = (slot // count) * count
        block = pl.ds(base, count)
        return [
            remote(seed_buf.at[block], seed_buf.at[block], 2 * step, partners[step]),
            remote(kv_buf.at[block], kv_buf.at[block], 2 * step + 1, partners[step]),
        ]

    flight = gather(0)
    for copy in flight:
        copy.start()
    sent = list(flight)
    shift_kv = [
        remote(keys, prior_k, 2 * bits, after),
        remote(values, prior_v, 2 * bits + 1, after),
    ]
    shift_state = [
        remote(tail_buf, tail_in, 2 * bits + 2, after),
        remote(state_buf, prior_state, 2 * bits + 3, after),
    ]

    first = me * rows
    start_col = starts_of_column(lengths[...], first, rows)
    start_row = starts_of_row(lengths[...], first, rows)
    same = (start_col == start_row) & (iota((rows, rows), 1) <= iota((rows, rows), 0))
    step_raw = raw[...]
    step_size = jnp.maximum(step_raw, 0.0) + jnp.log(1.0 + jnp.exp(-jnp.abs(step_raw)))
    pad = jnp.zeros((rows, 128 - heads), F32)
    falling = jnp.concatenate([-rate[...] * step_size, pad], axis=1)
    log_step = jnp.concatenate([jnp.log(step_size), pad], axis=1)
    same_f = same.astype(F32)
    same_b = same_f.astype(BF16)
    high = falling.astype(BF16)
    rest = falling - high.astype(F32)
    middle = rest.astype(BF16)
    low_part = (rest - middle.astype(F32)).astype(BF16)
    level = (
        jnp.dot(same_b, low_part, preferred_element_type=F32)
        + jnp.dot(same_b, middle, preferred_element_type=F32)
        + jnp.dot(same_b, high, preferred_element_type=F32)
    )
    last = level[rows - 1:rows, :]
    closing = start_col == start_col[rows - 1:rows, :]
    lo[...] = level
    lo_t[...] = jnp.transpose(level - log_step)
    weight[...] = jnp.where(closing, jnp.exp(jnp.minimum(last - level, 0.0) + log_step), 0.0)
    tail_buf[...] = jnp.broadcast_to(last, tail_buf.shape)
    for g in range(groups):
        write_t[g] = jnp.transpose(write[:, g * size:(g + 1) * size].astype(F32)).astype(BF16)
    low = iota((rows, 128), 1) < 64

    def state_pair(j, carry):
        lanes = pl.ds(pl.multiple_of(j * 128, 128), 128)
        scaled = x[:, lanes].astype(F32) * pair_of(weight[...], 2 * j, low)
        made = jnp.dot(
            write_t[j // pairs_per_group], scaled.astype(BF16), preferred_element_type=F32
        )
        state_buf[:, lanes] = made.astype(BF16)
        return carry

    lax.fori_loop(0, pairs, state_pair, 0, unroll=2)

    @pl.when(me < readers - 1)
    def _():
        for copy in shift_state + shift_kv:
            copy.start()

    half = rows // 2

    def group_step(g):
        at = slice(g * size, (g + 1) * size)
        inner[...] = nt(read[:, at], write[:, at]) * same_f

        def pair_step(k, carry):
            j = g * pairs_per_group + k
            lanes = pl.ds(pl.multiple_of(j * 128, 128), 128)
            for part in range(2):
                here = slice(part * half, (part + 1) * half)
                seen = (part + 1) * half
                x_seen = x[0:seen, lanes]
                products = []
                for side in range(2):
                    head = 2 * j + side
                    own = column_of(lo[here, :], head)
                    eight = lo_t[pl.ds(pl.multiple_of((j // 4) * 8, 8), 8), 0:seen]
                    chosen = iota((8, seen), 0) == lax.rem(j, 4) * 2 + side
                    other = jnp.sum(jnp.where(chosen, eight, 0.0), axis=0, keepdims=True)
                    mixing = inner[here, 0:seen] * jnp.exp(jnp.minimum(own - other, 80.0))
                    products.append(
                        jnp.dot(mixing.astype(BF16), x_seen, preferred_element_type=F32)
                    )
                low_here = iota((half, 128), 1) < 64
                gain = jnp.where(low_here, skip[2 * j], skip[2 * j + 1])
                y_out[here, lanes] = (
                    jnp.where(low_here, products[0], products[1])
                    + gain * x[here, lanes].astype(F32)
                )
            return carry

        lax.fori_loop(0, pairs_per_group, pair_step, 0)

    for index in range(max(bits, groups)):
        if index < groups:
            group_step(index)
        if index < bits:
            for copy in flight:
                copy.wait_recv()
            if index + 1 < bits:
                flight = gather(index + 1)
                for copy in flight:
                    copy.start()
                sent += flight
    for copy in sent:
        copy.wait_send()
    piece = prompt.shape[0]
    for j in range(readers):
        place = sum(((j >> (bits - 1 - step)) & 1) << step for step in range(bits))
        seed_out[j * piece:(j + 1) * piece, :] = seed_buf[place]
        both = kv_buf[place]
        pk_out[j * few:(j + 1) * few, :] = both[0:few]
        pv_out[j * few:(j + 1) * few, :] = both[few:2 * few]

    @pl.when(me == 0)
    def _():
        tail_in[...] = jnp.zeros_like(tail_in)

    @pl.when(me > 0)
    def _():
        for copy in shift_state + shift_kv:
            copy.wait_recv()

    @pl.when(me < readers - 1)
    def _():
        for copy in shift_state + shift_kv:
            copy.wait_send()

    carried = start_col < (me * rows).astype(F32)
    level = lo[...]
    to_prompt = jnp.exp(level + jnp.where(carried, tail_in[0:1, :], 0.0))
    to_state = jnp.where(carried, jnp.exp(level), 0.0)
    for g in range(groups):
        at = slice(g * per_group, (g + 1) * per_group)
        d_prompt[g] = to_prompt[:, at]
        d_state[g] = to_state[:, at]


def attend_kernel(
    group_size, lengths, q, pk, pv, near_k, near_v, own_k, own_v, out, bias
):
    rows = q.shape[0]
    prompts = pk.shape[0]
    half = rows // 2
    me = lax.axis_index("reader")
    first = me * rows

    @pl.when(pl.program_id(0) == 0)
    def _():
        start_col = starts_of_column(lengths[...], first, rows)
        start_row = starts_of_row(lengths[...], first - rows, 2 * rows)
        allowed = (
            (start_col == start_row)
            & (iota((rows, 2 * rows), 1) - rows <= iota((rows, 2 * rows), 0))
        )
        bias[...] = jnp.where(allowed, 0.0, -jnp.inf)

    k_near = jnp.where(me > 0, near_k[...].astype(F32), 0.0).astype(BF16)
    v_near = jnp.where(me > 0, near_v[...].astype(F32), 0.0).astype(BF16)
    k_all = jnp.concatenate([k_near, own_k[...]], axis=0)
    v_all = jnp.concatenate([v_near, own_v[...]], axis=0)
    scale = 1.0 / math.sqrt(HD)
    for part in range(2):
        here = slice(part * half, (part + 1) * half)
        near = slice(part * half, part * half + 3 * half)
        k_part = jnp.concatenate([pk[...], k_all[near]], axis=0)
        v_part = jnp.concatenate([pv[...], v_all[near]], axis=0)
        for j in range(group_size):
            at = slice(j * HD, (j + 1) * HD)
            scores = nt(q[here, at], k_part)
            scores = jnp.concatenate(
                [scores[:, :prompts], scores[:, prompts:] + bias[here, near]], axis=1
            )
            top = jnp.max(scores, axis=1, keepdims=True)
            weights = jnp.exp((scores - top) * scale)
            total = jnp.sum(weights, axis=1, keepdims=True)
            summed = jnp.dot(weights.astype(BF16), v_part, preferred_element_type=F32)
            out[here, at] = (summed / total).astype(BF16)


def finish_kernel(y, read, seed, state, d_prompt, d_state, gate, gain, out, v_buf):
    me = lax.axis_index("reader")
    rows, width = y.shape
    carried_state = jnp.where(me > 0, state[...].astype(F32), 0.0).astype(BF16)
    low = iota((rows, 128), 1) < 64
    square = jnp.zeros((rows, 128), F32)
    for k in range(width // 128):
        at = slice(k * 128, (k + 1) * 128)
        prompt_part = nt(read[...], seed[at, :])
        state_part = jnp.dot(read[...], carried_state[:, at], preferred_element_type=F32)
        by_prompt = jnp.where(
            low, d_prompt[0, :, 2 * k:2 * k + 1], d_prompt[0, :, 2 * k + 1:2 * k + 2]
        )
        by_state = jnp.where(
            low, d_state[0, :, 2 * k:2 * k + 1], d_state[0, :, 2 * k + 1:2 * k + 2]
        )
        mixed = y[:, at] + by_prompt * prompt_part + by_state * state_part
        u = gate[:, at].astype(F32)
        v = mixed * (u / (1.0 + jnp.exp(-u)))
        v_buf[:, at] = v
        square = square + v * v
    mean = jnp.sum(square, axis=1, keepdims=True) * (1.0 / width)
    factor = lax.rsqrt(mean + 1e-05)
    out[...] = (v_buf[...] * factor * gain[...]).astype(BF16)


def local(
    readers,
    answer_lengths, mixer_input, gate_input, state_write, state_read, step_raw, decay_rate,
    skip_gain, norm_gain, prompt_state, queries, answer_keys, answer_values, prompt_keys,
    prompt_values,
):
    rows, channels = mixer_input.shape
    heads = decay_rate.shape[0]
    size = prompt_state.shape[1]
    groups = state_write.shape[1] // size
    per_group = heads // groups
    kv_width = answer_keys.shape[1]
    bits = readers.bit_length() - 1
    lengths = answer_lengths.reshape(1, -1)
    few = prompt_keys.shape[0]
    prompts = readers * few
    piece = prompt_state.shape[0]
    vmem = pl.BlockSpec(memory_space=pltpu.VMEM)
    hbm = pl.BlockSpec(memory_space=pl.ANY)
    smem = pl.BlockSpec(memory_space=pltpu.SMEM)
    shape = jax.ShapeDtypeStruct
    y, seed, pk, pv, d_prompt, d_state, prior_k, prior_v, prior_state = pl.pallas_call(
        functools.partial(mix_kernel, readers, bits, groups),
        out_shape=(
            shape((rows, channels), F32),
            shape((readers * piece, size), BF16),
            shape((prompts, kv_width), BF16),
            shape((prompts, kv_width), BF16),
            shape((groups, rows, per_group), F32),
            shape((groups, rows, per_group), F32),
            shape((rows, kv_width), BF16),
            shape((rows, kv_width), BF16),
            shape((size, channels), BF16),
        ),
        in_specs=[vmem, vmem, vmem, vmem, vmem, vmem, smem, vmem, vmem, vmem, hbm, hbm],
        out_specs=(vmem, vmem, vmem, vmem, vmem, vmem, hbm, hbm, hbm),
        scratch_shapes=[
            pltpu.VMEM((readers, piece, size), BF16),
            pltpu.VMEM((readers, 2 * few, kv_width), BF16),
            pltpu.VMEM((size, channels), BF16),
            pltpu.VMEM((8, 128), F32),
            pltpu.VMEM((8, 128), F32),
            pltpu.VMEM((rows, 128), F32),
            pltpu.VMEM((128, rows), F32),
            pltpu.VMEM((rows, 128), F32),
            pltpu.VMEM((groups, size, rows), BF16),
            pltpu.VMEM((rows, rows), F32),
            pltpu.SemaphoreType.DMA((2 * bits + 4,)),
            pltpu.SemaphoreType.DMA((2 * bits + 4,)),
        ],
        compiler_params=pltpu.CompilerParams(
            collective_id=0, has_side_effects=True, vmem_limit_bytes=VMEM_LIMIT
        ),
        name="mix",
    )(
        lengths, mixer_input, state_write, state_read, step_raw, decay_rate.reshape(1, -1),
        skip_gain, prompt_state, prompt_keys, prompt_values, answer_keys, answer_values,
    )
    kv_heads = kv_width // HD
    group_size = queries.shape[1] // kv_width
    head_block = pl.BlockSpec((rows, HD), lambda k: (0, k))
    prompt_block = pl.BlockSpec((prompts, HD), lambda k: (0, k))
    q_block = pl.BlockSpec((rows, group_size * HD), lambda k: (0, k))
    attention_out = pl.pallas_call(
        functools.partial(attend_kernel, group_size),
        grid=(kv_heads,),
        out_shape=shape(queries.shape, BF16),
        in_specs=[
            pl.BlockSpec(lengths.shape, lambda k: (0, 0)), q_block, prompt_block, prompt_block,
            head_block, head_block, head_block, head_block,
        ],
        out_specs=q_block,
        scratch_shapes=[pltpu.VMEM((rows, 2 * rows), F32)],
        compiler_params=pltpu.CompilerParams(vmem_limit_bytes=VMEM_LIMIT),
        name="attend",
    )(lengths, queries, pk, pv, prior_k, prior_v, answer_keys, answer_values)
    width = channels // groups
    wide = pl.BlockSpec((rows, width), lambda g: (0, g))
    decay_block = pl.BlockSpec((1, rows, per_group), lambda g: (g, 0, 0))
    mixer_out = pl.pallas_call(
        finish_kernel,
        grid=(groups,),
        out_shape=shape((rows, channels), BF16),
        in_specs=[
            wide, pl.BlockSpec((rows, size), lambda g: (0, g)),
            pl.BlockSpec((width, size), lambda g: (g, 0)),
            pl.BlockSpec((size, width), lambda g: (0, g)),
            decay_block, decay_block, wide, pl.BlockSpec((1, width), lambda g: (0, g)),
        ],
        out_specs=wide,
        scratch_shapes=[pltpu.VMEM((rows, width), F32)],
        compiler_params=pltpu.CompilerParams(vmem_limit_bytes=VMEM_LIMIT),
        name="finish",
    )(
        y, state_read, seed, prior_state, d_prompt, d_state, gate_input,
        norm_gain.reshape(1, -1),
    )
    return (mixer_out, attention_out)


def solution(mesh):
    rows = P(("group", "reader"), None)
    in_specs = (P("group"), rows, rows, rows, rows, rows, P(), P(), P(), rows, rows, rows, rows, rows, rows)
    return jax.shard_map(
        functools.partial(local, mesh.shape["reader"]),
        mesh=mesh, in_specs=in_specs, out_specs=(rows, rows), check_vma=False,
    )
```

```python
import functools
import math

import jax
import jax.numpy as jnp
from jax import lax
from jax.experimental import pallas as pl
from jax.experimental.pallas import tpu as pltpu
from jax.sharding import PartitionSpec as P

HD = 128
F32 = jnp.float32
BF16 = jnp.bfloat16
MESH = pl.DeviceIdType.MESH
VMEM_LIMIT = 60 * 1024 * 1024
LOG2E = math.log2(math.e)


def iota(shape, axis):
    return lax.broadcasted_iota(jnp.int32, shape, axis)


def nt(a, b):
    return lax.dot_general(a, b, (((1,), (1,)), ((), ())), preferred_element_type=F32)


def starts_of_column(lengths_row, first, rows):
    n = lengths_row.shape[1]
    wide = jnp.broadcast_to(lengths_row.astype(F32), (8, n)).astype(BF16)
    ahead = (iota((n, n), 0) < iota((n, n), 1)).astype(F32).astype(BF16)
    starts = jnp.dot(wide, ahead, preferred_element_type=F32)[0:1, :]
    place = (iota((rows, n), 0) + first).astype(F32)
    return jnp.max(jnp.where(starts <= place, starts, -1.0), axis=1, keepdims=True)


def starts_of_row(lengths_row, first, columns):
    n = lengths_row.shape[1]
    wide = jnp.broadcast_to(lengths_row.astype(F32), (8, n)).astype(BF16)
    ahead = (iota((n, n), 1) < iota((n, n), 0)).astype(F32).astype(BF16)
    starts = nt(ahead, wide)[:, 0:1]
    place = (iota((n, columns), 1) + first).astype(F32)
    return jnp.max(jnp.where(starts <= place, starts, -1.0), axis=0, keepdims=True)


def column_of(value, index):
    lanes = iota(value.shape, 1)
    return jnp.sum(jnp.where(lanes == index, value, 0.0), axis=1, keepdims=True)


def halves_of(value):
    high = value.astype(BF16)
    return jnp.concatenate([high, (value - high.astype(F32)).astype(BF16)], axis=1)


def pick_of(j):
    head = lax.rem(iota((256, 128), 0), 128) - (iota((256, 128), 1) >= 64).astype(jnp.int32)
    return jnp.where(head == 2 * j, 1.0, 0.0).astype(BF16)


def mix_kernel(
    readers, bits, groups,
    lengths, x, write, read, raw, rate, skip, prompt, pkeys, pvalues, keys, values,
    gain, gate_in, q_in,
    mixer_out, attention_out,
    seed_buf, kv_buf, state_buf, state_prior, tail_buf, tail_in, lo, lo_t, weight, write_t,
    inner, y_out, gate, q, k_all, v_all, bias, d_prompt, d_state,
    send, recv, local_sem,
):
    rows = x.shape[0]
    heads = raw.shape[0]
    size = write.shape[1] // groups
    pairs = x.shape[1] // 128
    pairs_per_group = pairs // groups
    me = lax.axis_index("reader")
    bring_q = pltpu.make_async_copy(q_in, q, local_sem.at[0])
    bring_gate = pltpu.make_async_copy(gate_in, gate, local_sem.at[1])
    bring_q.start()
    bring_gate.start()
    after = lax.rem(me + 1, readers)
    ahead = lax.rem(me + readers - 1, readers)
    partners = []
    slot = 0
    for step in range(bits):
        unit = 1 << (bits - 1 - step)
        bit = lax.rem(me // unit, 2)
        partners.append(me + unit * (1 - 2 * bit))
        slot = slot + bit * (1 << step)
    barrier = pltpu.get_barrier_semaphore()
    for other in partners + [after, ahead]:
        pl.semaphore_signal(barrier, inc=1, device_id={"reader": other}, device_id_type=MESH)
    seed_buf[slot] = prompt[...].astype(BF16)
    few = pkeys.shape[0]
    kv_buf[slot] = jnp.concatenate([pkeys[...], pvalues[...]], axis=0)
    pl.semaphore_wait(barrier, bits + 2)

    def remote(source, target, index, other):
        return pltpu.make_async_remote_copy(
            src_ref=source, dst_ref=target, send_sem=send.at[index], recv_sem=recv.at[index],
            device_id={"reader": other}, device_id_type=MESH,
        )

    def gather(step):
        count = 1 << step
        base = (slot // count) * count
        block = pl.ds(base, count)
        return [
            remote(seed_buf.at[block], seed_buf.at[block], 2 * step, partners[step]),
            remote(kv_buf.at[block], kv_buf.at[block], 2 * step + 1, partners[step]),
        ]

    flights = [gather(step) for step in range(bits)]
    for copy in flights[0]:
        copy.start()

    def advance(step):
        for copy in flights[step]:
            copy.wait_recv()
        if step + 1 < bits:
            for copy in flights[step + 1]:
                copy.start()

    prompts = readers * few
    landing = pl.ds(prompts, rows)
    shift_kv = [
        remote(keys, k_all.at[landing], 2 * bits, after),
        remote(values, v_all.at[landing], 2 * bits + 1, after),
    ]
    shift_state = [
        remote(tail_buf, tail_in, 2 * bits + 2, after),
        remote(state_buf, state_prior, 2 * bits + 3, after),
    ]

    @pl.when(me < readers - 1)
    def _():
        for copy in shift_kv:
            copy.start()

    def launch_state():
        @pl.when(me < readers - 1)
        def _():
            for copy in shift_state:
                copy.start()

    k_all[prompts + rows:prompts + 2 * rows, :] = keys[...]
    v_all[prompts + rows:prompts + 2 * rows, :] = values[...]

    first = me * rows
    start_col = starts_of_column(lengths[...], first, rows)
    start_row = starts_of_row(lengths[...], first, rows)
    same = (start_col == start_row) & (iota((rows, rows), 1) <= iota((rows, rows), 0))
    step_raw = jnp.transpose(
        jnp.concatenate([raw[...], jnp.zeros((128 - raw.shape[0], rows), F32)], axis=0)
    )
    step_size = jnp.maximum(step_raw, 0.0) + jnp.log(1.0 + jnp.exp(-jnp.abs(step_raw)))
    rates = jnp.concatenate([rate[...], jnp.zeros((1, 128 - heads), F32)], axis=1)
    falling = -(LOG2E * rates) * step_size
    log_step = LOG2E * jnp.log(step_size)
    same_f = same.astype(F32)
    same_b = same_f.astype(BF16)
    high = falling.astype(BF16)
    rest = falling - high.astype(F32)
    middle = rest.astype(BF16)
    low_part = (rest - middle.astype(F32)).astype(BF16)
    level = (
        jnp.dot(same_b, low_part, preferred_element_type=F32)
        + jnp.dot(same_b, middle, preferred_element_type=F32)
        + jnp.dot(same_b, high, preferred_element_type=F32)
    )
    last = level[rows - 1:rows, :]
    closing = start_col == start_col[rows - 1:rows, :]
    lo[...] = level
    lo_t[...] = jnp.transpose(level - log_step)
    weight[...] = halves_of(
        jnp.where(closing, jnp.exp2(jnp.minimum(last - level, 0.0) + log_step), 0.0)
    )
    tail_buf[...] = jnp.broadcast_to(last, tail_buf.shape)
    for g in range(groups):
        write_t[g] = jnp.transpose(write[:, g * size:(g + 1) * size].astype(F32)).astype(BF16)

    def state_pair(j, carry):
        lanes = pl.ds(pl.multiple_of(j * 128, 128), 128)
        spread = jnp.dot(weight[...], pick_of(j), preferred_element_type=F32)
        scaled = x[:, lanes].astype(F32) * spread
        made = jnp.dot(
            write_t[j // pairs_per_group], scaled.astype(BF16), preferred_element_type=F32
        )
        state_buf[:, lanes] = made.astype(BF16)
        return carry

    lax.fori_loop(0, pairs // 2, state_pair, 0, unroll=2)
    advance(0)
    lax.fori_loop(pairs // 2, pairs, state_pair, 0, unroll=2)

    half = rows // 2

    def group_step(g):
        at = slice(g * size, (g + 1) * size)
        inner[...] = nt(read[:, at], write[:, at]) * same_f

        def pair_step(k, carry):
            j = g * pairs_per_group + k
            lanes = pl.ds(pl.multiple_of(j * 128, 128), 128)
            for part in range(2):
                here = slice(part * half, (part + 1) * half)
                seen = (part + 1) * half
                x_seen = x[0:seen, lanes]
                products = []
                for side in range(2):
                    head = 2 * j + side
                    own = column_of(lo[here, :], head)
                    eight = lo_t[pl.ds(pl.multiple_of((j // 4) * 8, 8), 8), 0:seen]
                    chosen = iota((8, seen), 0) == lax.rem(j, 4) * 2 + side
                    other = jnp.sum(jnp.where(chosen, eight, 0.0), axis=0, keepdims=True)
                    mixing = inner[here, 0:seen] * jnp.exp2(jnp.minimum(own - other, 115.0))
                    products.append(
                        jnp.dot(mixing.astype(BF16), x_seen, preferred_element_type=F32)
                    )
                low_here = iota((half, 128), 1) < 64
                gain = jnp.where(low_here, skip[2 * j], skip[2 * j + 1])
                y_out[here, lanes] = (
                    jnp.where(low_here, products[0], products[1])
                    + gain * x[here, lanes].astype(F32)
                )
            return carry

        lax.fori_loop(0, pairs_per_group, pair_step, 0, unroll=2)

    step = 1
    for g in range(groups):
        if g == 1 or g == groups - 1:
            advance(step)
            step += 1
        if g == groups - 1:
            launch_state()
        group_step(g)
    while step < bits:
        advance(step)
        step += 1
    for j in range(readers):
        place = sum(((j >> (bits - 1 - step)) & 1) << step for step in range(bits))
        both = kv_buf[place]
        k_all[j * few:(j + 1) * few, :] = both[0:few]
        v_all[j * few:(j + 1) * few, :] = both[few:2 * few]

    @pl.when(me == 0)
    def _():
        tail_in[...] = jnp.zeros_like(tail_in)
        state_prior[...] = jnp.zeros_like(state_prior)
        k_all[prompts:prompts + rows, :] = jnp.zeros((rows, keys.shape[1]), BF16)
        v_all[prompts:prompts + rows, :] = jnp.zeros((rows, keys.shape[1]), BF16)

    near_row = starts_of_row(lengths[...], first - rows, 2 * rows)
    allowed = (start_col == near_row) & (
        iota((rows, 2 * rows), 1) - rows <= iota((rows, 2 * rows), 0)
    )
    bias[...] = jnp.where(allowed, 0.0, -jnp.inf)
    bring_q.wait()

    @pl.when(me > 0)
    def _():
        for copy in shift_kv:
            copy.wait_recv()

    scale = LOG2E / math.sqrt(HD)
    kv_heads = keys.shape[1] // HD
    group_size = q.shape[1] // keys.shape[1]

    def attend(k, carry):
        kv_lanes = pl.ds(pl.multiple_of(k * HD, HD), HD)
        for part in range(2):
            here = slice(part * half, (part + 1) * half)
            near = slice(part * half, part * half + 3 * half)
            held = slice(prompts + part * half, prompts + part * half + 3 * half)
            for j in range(group_size):
                lanes = pl.ds(pl.multiple_of(k * group_size * HD + j * HD, HD), HD)
                q_part = q[here, lanes]
                far = nt(q_part, k_all[0:prompts, kv_lanes])
                close = nt(q_part, k_all[held, kv_lanes]) + bias[here, near]
                top = jnp.maximum(
                    jnp.max(far, axis=1, keepdims=True), jnp.max(close, axis=1, keepdims=True)
                )
                far = jnp.exp2((far - top) * scale)
                close = jnp.exp2((close - top) * scale)
                total = jnp.sum(far, axis=1, keepdims=True) + jnp.sum(
                    close, axis=1, keepdims=True
                )
                summed = jnp.dot(
                    far.astype(BF16), v_all[0:prompts, kv_lanes], preferred_element_type=F32
                ) + jnp.dot(
                    close.astype(BF16), v_all[held, kv_lanes], preferred_element_type=F32
                )
                attention_out[here, lanes] = (summed / total).astype(BF16)
        return carry

    lax.fori_loop(0, kv_heads, attend, 0)

    bring_gate.wait()

    @pl.when(me > 0)
    def _():
        for copy in shift_state:
            copy.wait_recv()

    carried = start_col < (me * rows).astype(F32)
    level = lo[...]
    d_prompt[...] = halves_of(jnp.exp2(level + jnp.where(carried, tail_in[0:1, :], 0.0)))
    d_state[...] = halves_of(jnp.where(carried, jnp.exp2(level), 0.0))
    width = x.shape[1] // groups
    piece = prompt.shape[0]
    for g in range(groups):
        read_part = read[:, g * size:(g + 1) * size]

        def finish(k, square):
            j = g * pairs_per_group + k
            lanes = pl.ds(pl.multiple_of(j * 128, 128), 128)
            row = j * 128
            owner = row // piece
            parts = []
            for one in range(max(1, 128 // piece)):
                number = owner + one
                place = 0
                for step in range(bits):
                    unit = 1 << (bits - 1 - step)
                    place = place + lax.rem(number // unit, 2) * (1 << step)
                if piece >= 128:
                    offset = pl.multiple_of(lax.rem(row, piece), 128)
                    parts.append(seed_buf[place, pl.ds(offset, 128), :])
                else:
                    parts.append(seed_buf[place])
            seed = parts[0] if len(parts) == 1 else jnp.concatenate(parts, axis=0)
            pick = pick_of(j)
            by_prompt = jnp.dot(d_prompt[...], pick, preferred_element_type=F32)
            by_state = jnp.dot(d_state[...], pick, preferred_element_type=F32)
            mixed = (
                y_out[:, lanes]
                + by_prompt * nt(read_part, seed)
                + by_state
                * jnp.dot(read_part, state_prior[:, lanes], preferred_element_type=F32)
            )
            u = gate[:, lanes].astype(F32)
            v = mixed * (u / (1.0 + jnp.exp(-u)))
            y_out[:, lanes] = v
            return square + v * v

        square = lax.fori_loop(0, pairs_per_group, finish, jnp.zeros((rows, 128), F32), unroll=2)
        mean = jnp.sum(square, axis=1, keepdims=True) * (1.0 / width)
        at = slice(g * width, (g + 1) * width)
        mixer_out[:, at] = (
            y_out[:, at] * lax.rsqrt(mean + 1e-05) * gain[:, at]
        ).astype(BF16)

    for flight in flights:
        for copy in flight:
            copy.wait_send()

    @pl.when(me < readers - 1)
    def _():
        for copy in shift_state + shift_kv:
            copy.wait_send()


def local(
    readers,
    answer_lengths, mixer_input, gate_input, state_write, state_read, step_raw, decay_rate,
    skip_gain, norm_gain, prompt_state, queries, answer_keys, answer_values, prompt_keys,
    prompt_values,
):
    rows, channels = mixer_input.shape
    heads = decay_rate.shape[0]
    size = prompt_state.shape[1]
    groups = state_write.shape[1] // size
    kv_width = answer_keys.shape[1]
    bits = readers.bit_length() - 1
    lengths = answer_lengths.reshape(1, -1)
    few = prompt_keys.shape[0]
    prompts = readers * few
    piece = prompt_state.shape[0]
    vmem = pl.BlockSpec(memory_space=pltpu.VMEM)
    hbm = pl.BlockSpec(memory_space=pl.ANY)
    smem = pl.BlockSpec(memory_space=pltpu.SMEM)
    shape = jax.ShapeDtypeStruct
    mixer_out, attention_out = pl.pallas_call(
        functools.partial(mix_kernel, readers, bits, groups),
        out_shape=(shape((rows, channels), BF16), shape(queries.shape, BF16)),
        in_specs=[
            vmem, vmem, vmem, vmem, vmem, vmem, smem, vmem, vmem, vmem, vmem, vmem,
            vmem, hbm, hbm,
        ],
        out_specs=(vmem, vmem),
        scratch_shapes=[
            pltpu.VMEM((readers, piece, size), BF16),
            pltpu.VMEM((readers, 2 * few, kv_width), BF16),
            pltpu.VMEM((size, channels), BF16),
            pltpu.VMEM((size, channels), BF16),
            pltpu.VMEM((8, 128), F32),
            pltpu.VMEM((8, 128), F32),
            pltpu.VMEM((rows, 128), F32),
            pltpu.VMEM((128, rows), F32),
            pltpu.VMEM((rows, 256), BF16),
            pltpu.VMEM((groups, size, rows), BF16),
            pltpu.VMEM((rows, rows), F32),
            pltpu.VMEM((rows, channels), F32),
            pltpu.VMEM((rows, channels), BF16),
            pltpu.VMEM(queries.shape, BF16),
            pltpu.VMEM((prompts + 2 * rows, kv_width), BF16),
            pltpu.VMEM((prompts + 2 * rows, kv_width), BF16),
            pltpu.VMEM((rows, 2 * rows), F32),
            pltpu.VMEM((rows, 256), BF16),
            pltpu.VMEM((rows, 256), BF16),
            pltpu.SemaphoreType.DMA((2 * bits + 4,)),
            pltpu.SemaphoreType.DMA((2 * bits + 4,)),
            pltpu.SemaphoreType.DMA((2,)),
        ],
        compiler_params=pltpu.CompilerParams(
            collective_id=0, has_side_effects=True, vmem_limit_bytes=VMEM_LIMIT
        ),
        name="mix",
    )(
        lengths, mixer_input, state_write, state_read, step_raw.T, decay_rate.reshape(1, -1),
        skip_gain, prompt_state, prompt_keys, prompt_values, answer_keys, answer_values,
        norm_gain.reshape(1, -1), gate_input, queries,
    )
    return (mixer_out, attention_out)


def solution(mesh):
    rows = P(("group", "reader"), None)
    in_specs = (P("group"), rows, rows, rows, rows, rows, P(), P(), P(), rows, rows, rows, rows, rows, rows)
    return jax.shard_map(
        functools.partial(local, mesh.shape["reader"]),
        mesh=mesh, in_specs=in_specs, out_specs=(rows, rows), check_vma=False,
    )
```
